32 devices in a mesh: grp: 4 (over y, core), dev: 8 (over z, x).
Axes of the slice: x: 2, y: 2, z: 4, core: 2. Of those that a mesh axis runs over, the one named last changes fastest.
Arguments:
- spectra: bfloat16 [96, 2, 16384], P(('grp', 'dev')), may hold values from -6 to 6
- partners: int32 [32, 8], P(('grp', 'dev')), may hold values from 0 to 7, all different within a row
- owners: int32 [256, 1], P(('grp', 'dev')), may hold values from 0 to 3; in each aligned block of 8 rows (0 to 7, 8 to 15, ...) at most 2 rows name the same one
- counts: int32 [4], replicated, may hold values from 12 to 24, as said below
- gain: float32 [8192], replicated, may hold values from 0.05 to 1
Outputs:
- coherence: bfloat16 [256, 3, 3, 16384], P(('grp', 'dev'))
The draws below stay inside these ranges and needn't reach their ends.
Inputs may be any that keep to these rules, and one draw needn't show every extreme that they name: `partners`: the 8 entries of a row are distinct. `owners`: of the 8 slots of one device, at most 2 have the same owner group, and exactly 2 do for some device. `counts`: some group has all 24 stations live and some has half of them.
All inputs are finite; a program needn't handle non-finite values.
Results may differ from the reference program's by a relative error of at most 0.0054.
Values may be sent and summed in bfloat16 or wider, within the bound.
A program may use at most 64 MiB of HBM per device.

```python
import math
import jax
import jax.numpy as jnp
import numpy as np
from jax import lax

F = 8192
S_DEV = 3
W = 2
P_DEV = 8
CAP = 2
GROUPS = 4
GROUP_ST = 24
STATIONS = 96
N_GRP = 4
N_DEV = 8


def draw_counts(key, part):
    values = jax.random.randint(key, (GROUPS,), GROUP_ST // 2, GROUP_ST + 1).astype(jnp.int32)
    order = jax.random.permutation(jax.random.fold_in(key, 7), GROUPS)
    values = values.at[order[0]].set(GROUP_ST)
    values = values.at[order[1]].set(GROUP_ST // 2)
    return values.astype(jnp.int32)


def shard_levels(own_key, shape, split, least, high):
    def one(axis_at, parts):
        steps = jax.random.uniform(jax.random.fold_in(jax.random.fold_in(own_key, 6), axis_at), (parts,), jnp.float32, least / len(split), high / len(split))
        return jnp.repeat(jnp.exp(steps), shape[axis_at] // parts).reshape((-1,) + (1,) * (len(shape) - axis_at - 1))

    factor_of = one(*split[0])
    for cut in split[1:]:
        factor_of = factor_of * one(*cut)
    return factor_of


def different_ones(key, rows, count, top, lift):
    sequence = jax.random.permutation(jax.random.fold_in(key, 1), count)
    boost = sequence
    for power in range(3):
        boost = boost * boost // count
    boost = boost * lift // count
    lots = jax.random.randint(jax.random.fold_in(key, 2), (rows, count), 0, 4096) + boost
    fixed_rows = jax.random.permutation(jax.random.fold_in(key, 3), rows)[jnp.arange(count) % rows]
    lots = jnp.where(jnp.arange(rows)[:, None] == fixed_rows[None, :], 1 << 14, lots)
    merit = lots * count + jnp.arange(count)
    return lax.top_k(merit.astype(jnp.int32), top)[1].astype(jnp.int32)


def routed_block(stream_key, own, number, rows, number_of, top, limit, slope):
    sequence = jax.random.permutation(stream_key, number_of)
    packed, ordinary = shares(number_of, rows * top, limit, slope, True), shares(number_of, rows * top, limit, slope, False)
    places = jnp.arange(number_of)

    def named(sizes, rotation):
        used = int((sizes > 0).sum())
        fixed = max(1, used // 4)
        shifted = fixed + (places - fixed + rotation * (used - fixed)) % max(1, number_of - fixed)
        return jnp.zeros((number_of,), jnp.int32).at[sequence[jnp.where(places < fixed, places, shifted)]].set(jnp.asarray(sizes, jnp.int32))

    sizes = jnp.where(number % 4 == 0, named(packed, number // 4), named(ordinary, number - number // 4 - 1))
    mixed = jax.random.permutation(jax.random.fold_in(own, 3), number_of)
    source_of, receiver = mixed[0:number_of // 2 * 2:2], mixed[1:number_of // 2 * 2:2]
    slack = jnp.minimum(sizes[source_of] - 1, limit - sizes[receiver]) // 2
    slack = jnp.where((source_of == sequence[0]) | (receiver == sequence[0]) | (sizes[receiver] == 0), 0, jnp.maximum(slack, 0))
    shifted = jax.random.randint(jax.random.fold_in(own, 4), (number_of // 2,), 0, 1 << 20) % (slack + 1)
    sizes = sizes.at[source_of].add(-shifted).at[receiver].add(shifted)
    items = jnp.searchsorted(jnp.cumsum(sizes), jnp.arange(rows * top), side="right").astype(jnp.int32)
    grid = items.reshape(top, rows).T
    grid = grid[jax.random.permutation(jax.random.fold_in(own, 1), rows)]
    rotation = jax.random.randint(jax.random.fold_in(own, 2), (rows, 1), 0, top)
    return jnp.take_along_axis(grid, (jnp.arange(top)[None, :] + rotation) % top, axis=1)


def shares(number_of, total, limit, slope, full):
    loads = [(1 << 20) // math.isqrt(grade ** slope) + 1 for grade in range(1, number_of + 1)]
    largest = limit if full else min(limit, max(-(-total // number_of), total * loads[0] // sum(loads)))
    least = 1 if total - largest >= number_of - 1 else 0
    holding, spare = [largest] + [least] * (number_of - 1), total - largest - least * (number_of - 1)
    while spare > 0:
        movable = [i for i in range(1, number_of) if holding[i] < largest] or [i for i in range(1, number_of) if holding[i] < limit]
        pool, budget = sum([loads[i] for i in movable]), spare
        for i in movable:
            extra = min(limit - holding[i], max(1, budget * loads[i] // pool), spare)
            holding[i] = holding[i] + extra
            spare = spare - extra
    return np.array(holding)


def noise(stream_key, dims, spread, most, shards=(), kind=jnp.bfloat16):
    array = jax.random.normal(stream_key, dims, jnp.float32) * spread
    if len(shards) > 0:
        array = shard_levels(stream_key, dims, shards, -0.22, 0.18) * array
    return jnp.clip(array, min=-most, max=most).astype(kind)


def setup_inputs(seed: int = 0) -> dict:
    key_list = jax.random.split(jax.random.key(seed), 6)
    spectra = noise(key_list[0], (STATIONS, W, 2 * F), 1.0, 6.0, ((0, 32),))
    partners = different_ones(key_list[1], (N_GRP * N_DEV), N_DEV, P_DEV, 0)
    owners_keys = jax.random.split(jax.random.fold_in(key_list[2], 1), (N_GRP * N_DEV * P_DEV) // P_DEV)
    owners_turns = jax.random.permutation(jax.random.fold_in(key_list[2], 3), (N_GRP * N_DEV * P_DEV) // P_DEV)
    owners = jax.vmap(lambda own, number: routed_block(jax.random.fold_in(key_list[2], 2), own, number, P_DEV, N_GRP, 1, CAP, 2))(owners_keys, owners_turns).reshape((N_GRP * N_DEV * P_DEV, 1))
    counts = draw_counts(jax.random.fold_in(key_list[5], 71), 0)
    gain = jnp.clip(jnp.exp(jax.random.uniform(key_list[4], (F,), jnp.float32, math.log(0.05), math.log(1.0))), 0.05, 1.0)
    return dict(spectra=spectra, partners=partners, owners=owners, counts=counts, gain=gain)


EPS = 1e-06

def cross_spectra(own, part):
    half = own.shape[-1] // 2
    own_f = own.astype(jnp.float32)
    part_f = part.astype(jnp.float32)
    a_own, b_own = (own_f[..., :half], own_f[..., half:])
    a_part, b_part = (part_f[..., :half], part_f[..., half:])
    real_part = jnp.einsum('...iwf,...jwf->...ijf', a_own, a_part) + jnp.einsum('...iwf,...jwf->...ijf', b_own, b_part)
    imag_part = jnp.einsum('...iwf,...jwf->...ijf', b_own, a_part) - jnp.einsum('...iwf,...jwf->...ijf', a_own, b_part)
    return jnp.concatenate([real_part, imag_part], axis=-1)

def energies(block, gain_two):
    values = block.astype(jnp.float32)
    total = lax.optimization_barrier(jnp.sum(gain_two * values * values, axis=(-2, -1)))
    return total / (values.shape[-2] * values.shape[-1])

def pair_output(own, part, gain_two):
    stack = (cross_spectra(own, part) * gain_two).astype(jnp.bfloat16)
    stack = lax.optimization_barrier(stack).astype(jnp.float32)
    e_own = energies(own, gain_two).astype(jnp.bfloat16)
    e_part = energies(part, gain_two).astype(jnp.bfloat16)
    e_own, e_part = lax.optimization_barrier((e_own, e_part))
    e_own = e_own.astype(jnp.float32)
    e_part = e_part.astype(jnp.float32)
    denom = own.shape[-2] * jnp.sqrt((e_own[..., :, None] + EPS) * (e_part[..., None, :] + EPS))
    return (stack / denom[..., None]).astype(jnp.bfloat16)

def reference(spectra, partners, owners, counts, gain):
    gain_two = jnp.concatenate([gain, gain])
    station = jnp.arange(STATIONS, dtype=jnp.int32)
    group_of = station // GROUP_ST
    live = station % GROUP_ST < counts[group_of]
    masked = spectra * live.astype(jnp.bfloat16)[:, None, None]
    owner = owners.reshape(N_GRP * N_DEV, P_DEV)
    slot = jnp.arange(P_DEV, dtype=jnp.int32)
    earlier = slot[None, :] < slot[:, None]
    same = owner[:, :, None] == owner[:, None, :]
    rank = lax.optimization_barrier(jnp.sum((same & earlier[None]).astype(jnp.int32), axis=-1)).astype(jnp.int32)
    start_out = jnp.zeros((N_GRP * N_DEV * N_GRP * CAP, S_DEV, S_DEV, 2 * F), jnp.bfloat16)

    def step(source, result):
        source = jnp.asarray(source).astype(jnp.int32)
        group = source // N_DEV
        device = source % N_DEV
        own = lax.dynamic_slice_in_dim(masked, (source * S_DEV).astype(jnp.int32), S_DEV, 0)
        blocks = partners[source]

        def take(block):
            begin = ((group * N_DEV + block) * S_DEV).astype(jnp.int32)
            return lax.dynamic_slice_in_dim(masked, begin, S_DEV, 0)
        part = jax.vmap(take)(blocks)
        own_all = jnp.broadcast_to(own, part.shape)
        values = pair_output(own_all, part, gain_two)
        dest = (((owner[source] * N_DEV + device) * N_GRP + group) * CAP + rank[source]).astype(jnp.int32)
        return result.at[dest].set(values)
    return lax.fori_loop(jnp.int32(0), jnp.int32(N_GRP * N_DEV), step, start_out)
```

```python
import functools

import jax
import jax.numpy as jnp
from jax import lax
from jax.experimental import pallas as pl
from jax.experimental.pallas import tpu as pltpu
from jax.sharding import PartitionSpec as P

CAP = 2
EPS = 1e-06
MAJOR = 4
CHUNKS = 4
LANES = 128


def kernel(groups, n_dev, windows, x_ref, part_ref, owner_ref, gain_ref, out_ref, *scratch):
    bufs = scratch[:CHUNKS]
    (send, part_in, own_in, acc_own, acc_part, inv_ref,
     zs, zr, xs, xr, os_, or_, ps, pr) = scratch[CHUNKS:]
    minor = n_dev // MAJOR
    per_dev = acc_own.shape[0]
    rows_out = groups * CAP
    height = gain_ref.shape[1]
    block_rows = x_ref.shape[1]
    slots = part_ref.shape[1]
    me_g = lax.axis_index("grp")
    me_d = lax.axis_index("dev")
    z = me_d // minor
    x = me_d % minor

    def other_group(delta):
        return lax.rem(me_g + delta, groups)

    def other_minor(delta):
        return z * minor + lax.rem(x + delta, minor)

    barrier = pltpu.get_barrier_semaphore()

    def greet(**where):
        pl.semaphore_signal(barrier, inc=1, device_id=where, device_id_type=pl.DeviceIdType.MESH)

    for delta in range(1, groups):
        greet(grp=other_group(delta))
    for delta in range(1, minor):
        greet(dev=other_minor(delta))

    @pl.when(z > 0)
    def _():
        greet(dev=me_d - minor)

    @pl.when(z < MAJOR - 1)
    def _():
        greet(dev=me_d + minor)

    for c in range(CHUNKS):
        bufs[c][me_d] = x_ref[c]
    own_in[me_g] = x_ref[...]
    acc_own[...] = jnp.zeros_like(acc_own)
    acc_part[...] = jnp.zeros_like(acc_part)

    owners = [owner_ref[p, 0] for p in range(slots)]
    partners = [part_ref[0, p] for p in range(slots)]
    dests = []
    for p in range(slots):
        rank = jnp.int32(0)
        for before in range(p):
            rank = rank + jnp.where(owners[before] == owners[p], 1, 0)
        dests.append(owners[p] * CAP + rank)
    chosen, filled = [], []
    for k in range(rows_out):
        index, used = jnp.int32(0), jnp.int32(0)
        for p in range(slots):
            index = jnp.where(dests[p] == k, partners[p], index)
            used = jnp.where(dests[p] == k, 1, used)
        chosen.append(index)
        filled.append(used)

    neighbours = jnp.where(z > 0, 1, 0) + jnp.where(z < MAJOR - 1, 1, 0)
    pl.semaphore_wait(barrier, groups - 1 + minor - 1 + neighbours)

    def remote(src, dst, send_sem, recv_sem, **where):
        return pltpu.make_async_remote_copy(
            src_ref=src, dst_ref=dst, send_sem=send_sem, recv_sem=recv_sem,
            device_id=where, device_id_type=pl.DeviceIdType.MESH)

    def own_copy(delta):
        return remote(x_ref, own_in.at[me_g], os_.at[delta - 1], or_.at[delta - 1],
                      grp=other_group(delta))

    def part_copy(delta, c):
        return remote(send.at[other_group(delta), c], part_in.at[me_g, c],
                      ps.at[delta - 1, c], pr.at[delta - 1, c], grp=other_group(delta))

    def chain_copy(up, dist, c, block):
        ref = bufs[c].at[block]
        way = 0 if up else 1
        target = me_d + minor if up else me_d - minor
        return remote(ref, ref, zs.at[way, dist, c], zr.at[way, dist, c], dev=target)

    def side_copy(number, delta, c, block):
        ref = bufs[c].at[block]
        return remote(ref, ref, xs.at[number, delta - 1, c], xr.at[number, delta - 1, c],
                      dev=other_minor(delta))

    def sources():
        yield None, 0, 0, None, me_d
        for dist in range(1, MAJOR):
            yield True, dist, dist, z >= dist, me_d - dist * minor
            yield False, dist, MAJOR - 1 + dist, z + dist < MAJOR, me_d + dist * minor

    def guarded(condition, run):
        if condition is None:
            run()
        else:
            pl.when(condition)(run)

    def each_send(way, dist, number, block, c, act):
        if dist + 1 < MAJOR:
            if way is None or way:
                guarded(z < MAJOR - 1, lambda: act(chain_copy(True, dist + 1, c, block)))
            if way is None or not way:
                guarded(z > 0, lambda: act(chain_copy(False, dist + 1, c, block)))
        for delta in range(1, minor):
            act(side_copy(number, delta, c, block))

    for delta in range(1, groups):
        own_copy(delta).start()

    def hop(at_dist, c):
        for way, dist, number, condition, block in sources():
            if dist != at_dist:
                continue

            def run(way=way, dist=dist, number=number, block=block):
                if dist:
                    chain_copy(way, dist, c, block).wait_recv()
                each_send(way, dist, number, block, c, lambda copy: copy.start())

            guarded(condition, run)

    def forward(c):
        for way, dist, number, condition, block in sources():
            def run(number=number, block=block):
                for delta in range(1, minor):
                    side_copy(number, delta, c, block).wait_recv()

            guarded(condition, run)
        for o in range(groups):
            for r in range(CAP):
                k = o * CAP + r
                taken = bufs[c][chosen[k]]
                taken = jnp.where(filled[k] > 0, taken, jnp.zeros_like(taken))
                send[o, c, pl.ds(r * block_rows, block_rows)] = taken
        for delta in range(1, groups):
            part_copy(delta, c).start()
        part_in[me_g, c] = send[me_g, c]

    def compute(c):
        if c == 0:
            for delta in range(1, groups):
                own_copy(delta).wait_recv()
        for delta in range(1, groups):
            part_copy(delta, c).wait_recv()
        gain = gain_ref[c]

        def one(row, carry):
            g = row // CAP
            r = row % CAP

            def piece(load, s, w, half):
                return load(((s * windows + w) * 2 + half) * height).astype(jnp.float32)

            def from_own(at):
                return own_in[g, c, pl.ds(at, height)]

            def from_part(at):
                base = pl.multiple_of(r * block_rows, block_rows)
                return part_in[g, c, pl.ds(base + at, height)]

            parts = [[[piece(from_part, s, w, h) for h in range(2)] for w in range(windows)]
                     for s in range(per_dev)]
            for s in range(per_dev):
                total = sum(v * v for pair in parts[s] for v in pair)
                acc_part[s, row] += total * gain
            for i in range(per_dev):
                own = [[piece(from_own, i, w, h) for h in range(2)] for w in range(windows)]
                total = sum(v * v for pair in own for v in pair)
                acc_own[i, row] += total * gain
                for j in range(per_dev):
                    real = sum(own[w][0] * parts[j][w][0] + own[w][1] * parts[j][w][1]
                               for w in range(windows))
                    imag = sum(own[w][1] * parts[j][w][0] - own[w][0] * parts[j][w][1]
                               for w in range(windows))
                    n = i * per_dev + j
                    out_ref[row, n, 0, c] = (real * gain).astype(jnp.bfloat16)
                    out_ref[row, n, 1, c] = (imag * gain).astype(jnp.bfloat16)
            return carry

        lax.fori_loop(0, rows_out, one, 0)

    for t in range(CHUNKS + MAJOR + 1):
        for dist in range(MAJOR):
            if 0 <= t - dist < CHUNKS:
                hop(dist, t - dist)
        if 0 <= t - MAJOR + 1 < CHUNKS:
            forward(t - MAJOR + 1)
        if 0 <= t - MAJOR - 1 < CHUNKS:
            compute(t - MAJOR - 1)

    entries = windows * 2 * CHUNKS * height * LANES

    def energy(acc, s):
        value = jnp.sum(jnp.sum(acc[s], axis=1), axis=-1, keepdims=True) / entries
        return value.astype(jnp.bfloat16).astype(jnp.float32) + EPS

    own_e = [energy(acc_own, s) for s in range(per_dev)]
    part_e = [energy(acc_part, s) for s in range(per_dev)]
    for i in range(per_dev):
        for j in range(per_dev):
            inverse = 1.0 / (windows * jnp.sqrt(own_e[i] * part_e[j]))
            inv_ref[i * per_dev + j] = jnp.broadcast_to(inverse, inv_ref.shape[1:])

    def scale(row, carry):
        for n in range(per_dev * per_dev):
            factor = inv_ref[n, pl.ds(row, 1)]
            for half in range(2):
                for c in range(CHUNKS):
                    stack = out_ref[row, n, half, c].astype(jnp.float32)
                    out_ref[row, n, half, c] = (stack * factor).astype(jnp.bfloat16)
        return carry

    lax.fori_loop(0, rows_out, scale, 0)

    for delta in range(1, groups):
        own_copy(delta).wait_send()
    for c in range(CHUNKS):
        for way, dist, number, condition, block in sources():
            def run(way=way, dist=dist, number=number, block=block):
                each_send(way, dist, number, block, c, lambda copy: copy.wait_send())

            guarded(condition, run)
        for delta in range(1, groups):
            part_copy(delta, c).wait_send()


def body(spectra, partners, owners, counts, gain):
    groups = lax.axis_size("grp")
    n_dev = lax.axis_size("dev")
    group = lax.axis_index("grp")
    device = lax.axis_index("dev")
    per_dev, windows, full = spectra.shape
    minor = n_dev // MAJOR
    height = full // 2 // CHUNKS // LANES
    group_count = jnp.sum(jnp.where(jnp.arange(groups) == group, counts, 0))
    station = device * per_dev + jnp.arange(per_dev, dtype=jnp.int32)
    live = (station < group_count).astype(jnp.bfloat16)
    masked = spectra * live[:, None, None]
    cut = masked.reshape(per_dev * windows * 2, CHUNKS, height, LANES).transpose(1, 0, 2, 3)
    block_rows = per_dev * windows * 2 * height
    cut = cut.reshape(CHUNKS, block_rows, LANES)
    rows = groups * CAP
    bf16, f32 = jnp.bfloat16, jnp.float32
    pairs = per_dev * per_dev
    dma = pltpu.SemaphoreType.DMA
    vmem = pl.BlockSpec(memory_space=pltpu.VMEM)
    smem = pl.BlockSpec(memory_space=pltpu.SMEM)
    out = pl.pallas_call(
        functools.partial(kernel, groups, n_dev, windows),
        out_shape=jax.ShapeDtypeStruct((rows, pairs, 2, CHUNKS, height, LANES), bf16),
        in_specs=[vmem, smem, smem, vmem],
        out_specs=vmem,
        scratch_shapes=[pltpu.VMEM((n_dev, block_rows, LANES), bf16)] * CHUNKS + [
            pltpu.VMEM((groups, CHUNKS, CAP * block_rows, LANES), bf16),
            pltpu.VMEM((groups, CHUNKS, CAP * block_rows, LANES), bf16),
            pltpu.VMEM((groups, CHUNKS, block_rows, LANES), bf16),
            pltpu.VMEM((per_dev, rows, height, LANES), f32),
            pltpu.VMEM((per_dev, rows, height, LANES), f32),
            pltpu.VMEM((pairs, rows, LANES), f32),
            dma((2, MAJOR, CHUNKS)),
            dma((2, MAJOR, CHUNKS)),
            dma((2 * MAJOR - 1, max(minor - 1, 1), CHUNKS)),
            dma((2 * MAJOR - 1, max(minor - 1, 1), CHUNKS)),
            dma((groups - 1,)),
            dma((groups - 1,)),
            dma((groups - 1, CHUNKS)),
            dma((groups - 1, CHUNKS)),
        ],
        compiler_params=pltpu.CompilerParams(
            collective_id=0, has_side_effects=True, vmem_limit_bytes=40 * 1024 * 1024),
    )(cut, partners, owners, gain.reshape(CHUNKS, height, LANES))
    return out.reshape(rows, per_dev, per_dev, full)


def solution(mesh):
    in_specs = (
        P(("grp", "dev"), None, None),
        P(("grp", "dev"), None),
        P(("grp", "dev"), None),
        P(),
        P(),
    )
    out_specs = P(("grp", "dev"), None, None, None)
    return jax.shard_map(body, mesh=mesh, in_specs=in_specs, out_specs=out_specs, check_vma=False)
```
